256 devices in a mesh: cuts: 128 (over y, z, x), site: 2 (over core).
Axes of the slice: x: 4, y: 4, z: 8, core: 2. Of those that a mesh axis runs over, the one named last changes fastest.
Arguments:
- field: float32 [128, 2048], P('cuts'), may hold values from -4 to 4
- momenta: float32 [128, 2048], P('cuts'), may hold values from -4 to 4
- start_force: float32 [128, 2048], P('cuts'), may hold values from -4 to 4
- green: bfloat16 [128, 2048, 2048], P('cuts', 'site'), as said below
- forward_prop: bfloat16 [2048, 2048], P('site')
- back_prop: bfloat16 [2048, 2048], P('site')
- accept: int32 [128], P('cuts'), may hold values from 0 to 1
Outputs:
- new_field: float32 [128, 2048], P('cuts')
- new_momenta: float32 [128, 2048], P('cuts')
- new_force: float32 [128, 2048], P('cuts')
- energy_change: float32 [1], replicated
The draws below stay inside these ranges and needn't reach their ends.
Inputs may be any that keep to these rules, and one draw needn't show every extreme that they name: green has a diagonal of 0.2 to 0.8 plus full-rank off-diagonal entries; the propagators are the identity plus full-rank entries.
All inputs are finite; a program needn't handle non-finite values.
Results may differ from the reference program's by a relative error of at most 0.0029.
Values may be sent and summed in bfloat16 or wider, within the bound.
No kernel may reach another device: no remote copies, remote signals or barrier semaphores. Data moves between devices by JAX's collectives and lax.ppermute only.
A program may use at most 128 MiB of HBM per device.

```python
import jax
import jax.numpy as jnp
from jax import lax

N = 2048
SLICES = 128


def draw_green(key, part):
    noise = jax.random.normal(jax.random.fold_in(key, 11), (SLICES, N, N), jnp.float32) * (1.0 / N ** 0.5)
    middle = jax.random.uniform(jax.random.fold_in(key, 12), (SLICES, N, 1), jnp.float32, 0.2, 0.8)
    unit = (jnp.arange(N)[:, None] == jnp.arange(N)[None, :]).astype(jnp.float32)
    return (noise + middle * unit[None, :, :]).astype(jnp.bfloat16)


def propagator(key, salt):
    noise = jax.random.normal(jax.random.fold_in(key, salt), (N, N), jnp.float32) * (1.0 / N ** 0.5)
    unit = (jnp.arange(N)[:, None] == jnp.arange(N)[None, :]).astype(jnp.float32)
    return (noise + unit).astype(jnp.bfloat16)


def draw_forward_prop(key, part):
    return propagator(key, 21)


def draw_back_prop(key, part):
    return propagator(key, 22)


def touch_ends(array, stream_key, smallest, top_value):
    longest = array.shape.index(max(array.shape))
    spots = []
    for shift in (0, 1):
        where = [jax.random.randint(jax.random.fold_in(stream_key, axis), (), 0, length) for axis, length in enumerate(array.shape)]
        where[longest] = (where[longest] + shift) % array.shape[longest]
        spots.append(tuple(where))
    return array.at[spots[0]].set(smallest).at[spots[1]].set(top_value)


def block_scale(rng, dims, cuts, least, high):
    gain, own = 1.0, jax.random.fold_in(rng, 6)
    for dim, blocks in cuts:
        steps = jnp.exp(jax.random.uniform(jax.random.fold_in(own, dim), (blocks,), jnp.float32, least / len(cuts), high / len(cuts)))
        gain = gain * jnp.repeat(steps, dims[dim] // blocks).reshape([-1 if axis == dim else 1 for axis in range(len(dims))])
    return gain


def bell_draw(key, dims, width, reach, cuts=(), kind=jnp.bfloat16):
    loudness = block_scale(key, dims, cuts, -0.22, 0.18) if cuts else 1.0
    values = jax.random.normal(key, dims, jnp.float32) * width * loudness
    return jnp.minimum(jnp.maximum(values, -reach), reach).astype(kind)


def setup_inputs(seed: int = 0) -> dict:
    arg_keys = jax.random.split(jax.random.key(seed), 8)
    field = bell_draw(arg_keys[0], (SLICES, N), 1.0, 4.0, ((0, 128),), jnp.float32)
    momenta = bell_draw(arg_keys[1], (SLICES, N), 1.0, 4.0, ((0, 128),), jnp.float32)
    start_force = bell_draw(arg_keys[2], (SLICES, N), 1.0, 4.0, ((0, 128),), jnp.float32)
    green = draw_green(jax.random.fold_in(arg_keys[7], 71), 0)
    forward_prop = draw_forward_prop(jax.random.fold_in(arg_keys[7], 71), 0)
    back_prop = draw_back_prop(jax.random.fold_in(arg_keys[7], 71), 0)
    accept = touch_ends(jax.random.randint(arg_keys[6], (SLICES,), 0, 2), jax.random.fold_in(arg_keys[6], 1), 0, 1).astype(jnp.int32)
    return {"field": field, "momenta": momenta, "start_force": start_force, "green": green, "forward_prop": forward_prop, "back_prop": back_prop, "accept": accept}


coupling = 0.5
stepsize = 0.2

def reference(field, momenta, start_force, green, forward_prop, back_prop, accept):
    half = momenta - 0.5 * stepsize * start_force
    trial = field + stepsize * half
    previous = jnp.roll(green, 1, axis=0)
    back_wide = back_prop.astype(jnp.float32)

    def one_slice(inputs):
        before, phase = inputs
        scaled = (jnp.exp(coupling * phase)[:, None] * before.astype(jnp.float32)).astype(jnp.bfloat16)
        wrapped = jnp.dot(forward_prop, scaled, preferred_element_type=jnp.float32)
        return lax.optimization_barrier(jnp.sum(wrapped * (jnp.exp(-coupling * phase)[None, :] * back_wide), axis=1))
    diagonal = lax.map(one_slice, (previous, trial))
    new_force = trial - 2.0 * coupling * (1.0 - 2.0 * diagonal)
    new_momenta = half - 0.5 * stepsize * new_force
    total = jnp.sum(new_momenta * new_momenta) + jnp.sum(trial * trial) - jnp.sum(momenta * momenta) - jnp.sum(field * field)
    change = total / (2.0 * jnp.sqrt(jnp.float32(SLICES * N)))
    new_field = jnp.where(accept[:, None] == 1, trial, field)
    return (new_field, new_momenta, new_force, jnp.reshape(change, (1,)).astype(jnp.float32))
```

```python
import jax
import jax.numpy as jnp
from jax import lax
from jax.experimental import pallas as pl
from jax.experimental.pallas import tpu as pltpu
from jax.sharding import Mesh
from jax.sharding import PartitionSpec as P

CUTS = ("cuts_0", "cuts_1", "cuts_2")
ALL = (*CUTS, "site")
LANES = 128
COLUMNS = 256

coupling = 0.5
stepsize = 0.2


def stepped(field, momenta, start_force):
    half = momenta - 0.5 * stepsize * start_force
    return field + stepsize * half, half


def moved_by(trial, half, diagonal):
    force = trial - 2.0 * coupling * (1.0 - 2.0 * diagonal)
    return force, half - 0.5 * stepsize * force


def diagonal_kernel(nxt_ref, field_ref, momenta_ref, start_ref, near_ref, far_ref, forward_ref, back_ref,
                    diag_ref, part_ref, scaled, acc):
    rows, sites = forward_ref.shape
    blocks = rows // LANES
    site = lax.axis_index("site")
    first = site == 0

    def by_rows(row):
        whole = jnp.reshape(row, (2 * blocks, LANES))
        own = jnp.where(first, whole[:blocks], whole[blocks:])
        return own, jnp.where(first, whole[blocks:], whole[:blocks])

    growth = jnp.exp(coupling * nxt_ref[0:1, :])
    factors = jnp.transpose(jnp.concatenate(by_rows(growth), axis=0))
    near_at = pl.multiple_of(site * rows, LANES)
    far_at = pl.multiple_of((1 - site) * rows, LANES)

    def scale(j):
        span = pl.ds(j * COLUMNS, COLUMNS)
        for b in range(2 * blocks):
            source = near_ref if b < blocks else far_ref
            block = source[pl.ds(b % blocks * LANES, LANES), span].astype(jnp.float32)
            scaled[j % 2, pl.ds(b * LANES, LANES), :] = (factors[:, b : b + 1] * block).astype(jnp.bfloat16)

    steps = sites // COLUMNS
    scale(0)
    for j in range(steps):
        span = pl.ds(j * COLUMNS, COLUMNS)
        if j + 1 < steps:
            scale(j + 1)
        shrink = jnp.exp(-coupling * nxt_ref[0:1, span])
        wrapped = jnp.dot(
            forward_ref[:, pl.ds(near_at, rows)], scaled[j % 2, :rows, :], preferred_element_type=jnp.float32
        ) + jnp.dot(
            forward_ref[:, pl.ds(far_at, rows)], scaled[j % 2, rows:, :], preferred_element_type=jnp.float32
        )
        product = wrapped * (shrink * back_ref[:, span].astype(jnp.float32))
        part = product[:, :LANES] + product[:, LANES:]
        if j == 0:
            acc[...] = part
        else:
            acc[...] += part
    diag = jnp.concatenate(
        [
            jnp.sum(jnp.transpose(acc[pl.ds(b * LANES, LANES), :]), axis=0, keepdims=True)
            for b in range(blocks)
        ],
        axis=0,
    )
    diag_ref[...] = diag
    moved = moved_by(by_rows(nxt_ref[0:1, :])[0], by_rows(nxt_ref[1:2, :])[0], diag)[1]
    field, momenta = field_ref[...], momenta_ref[...]
    trial = stepped(field, momenta, start_ref[...])[0]
    total = jnp.sum(moved * moved) + 0.5 * jnp.sum(trial * trial - momenta * momenta - field * field)
    part_ref[...] = jnp.full(part_ref.shape, total, jnp.float32)


def closing_kernel(scale, accept_ref, field_ref, momenta_ref, start_ref, straight_ref, crossed_ref, parts_ref,
                   new_field_ref, new_momenta_ref, new_force_ref, change_ref):
    first = lax.axis_index("site") == 0
    straight, crossed = straight_ref[...], crossed_ref[...]
    diagonal = jnp.concatenate(
        [jnp.where(first, straight, crossed), jnp.where(first, crossed, straight)], axis=0
    )
    field = field_ref[...]
    trial, half = stepped(field, momenta_ref[...], start_ref[...])
    force, moved = moved_by(trial, half, jnp.reshape(diagonal, field.shape))
    new_force_ref[...] = force
    new_momenta_ref[...] = moved
    new_field_ref[...] = jnp.where(accept_ref[0] == 1, trial, field)
    change_ref[0] = scale * jnp.sum(parts_ref[...])


def on_device(field, momenta, start_force, green, forward_prop, back_prop, accept):
    near = green[0]
    rows, sites = near.shape
    devices = lax.axis_size(ALL)
    cuts = lax.axis_size(CUTS)
    row = jax.ShapeDtypeStruct((1, sites), jnp.float32)
    vmem = pl.BlockSpec(memory_space=pltpu.VMEM)
    smem = pl.BlockSpec(memory_space=pltpu.SMEM)

    def held(x):
        return pltpu.with_memory_space_constraint(x, pltpu.VMEM)

    far = lax.ppermute(near, "site", [(0, 1), (1, 0)])
    nxt = lax.ppermute(
        jnp.concatenate(stepped(field, momenta, start_force), axis=0),
        CUTS,
        [(i, (i - 1) % cuts) for i in range(cuts)],
    )
    diag, part = pl.pallas_call(
        diagonal_kernel,
        out_shape=(
            jax.ShapeDtypeStruct((rows // LANES, LANES), jnp.float32),
            jax.ShapeDtypeStruct((devices, LANES), jnp.float32),
        ),
        in_specs=[vmem] * 8,
        out_specs=(vmem, vmem),
        scratch_shapes=[
            pltpu.VMEM((2, sites, COLUMNS), jnp.bfloat16),
            pltpu.VMEM((rows, LANES), jnp.float32),
        ],
        compiler_params=pltpu.CompilerParams(vmem_limit_bytes=32 * 1024 * 1024),
        cost_estimate=pl.CostEstimate(
            flops=2 * rows * sites * sites, bytes_accessed=8 * rows * sites, transcendentals=2 * sites
        ),
        name="diagonal",
    )(*map(held, (nxt, field, momenta, start_force, near, far, forward_prop, back_prop)))
    straight = lax.ppermute(diag, ALL, [(i, (i + 2) % devices) for i in range(devices)])
    crossed = lax.ppermute(diag, ALL, [(i, ((i + 2) % devices) ^ 1) for i in range(devices)])
    parts = lax.all_to_all(part, ALL, split_axis=0, concat_axis=0, tiled=True)
    scale = 1.0 / (2.0 * (cuts * sites) ** 0.5) / LANES
    new_field, new_momenta, new_force, change = pl.pallas_call(
        lambda *refs: closing_kernel(scale, *refs),
        out_shape=(row, row, row, jax.ShapeDtypeStruct((1,), jnp.float32)),
        in_specs=[smem] + [vmem] * 6,
        out_specs=(vmem, vmem, vmem, smem),
        compiler_params=pltpu.CompilerParams(vmem_limit_bytes=4 * 1024 * 1024),
        name="closing",
    )(accept, *map(held, (field, momenta, start_force, straight, crossed, parts)))
    return new_field, new_momenta, new_force, change


def solution(mesh):
    finer = Mesh(
        mesh.devices.reshape(4, 8, 4, mesh.shape["site"]), ("cuts_0", "cuts_1", "cuts_2", "site")
    )
    in_specs = (
        P(CUTS, None),
        P(CUTS, None),
        P(CUTS, None),
        P(CUTS, "site", None),
        P("site", None),
        P("site", None),
        P(CUTS),
    )
    out_specs = (P(CUTS, None), P(CUTS, None), P(CUTS, None), P())
    return jax.shard_map(
        on_device, mesh=finer, in_specs=in_specs, out_specs=out_specs, check_vma=False
    )
```

```python
import jax
import jax.numpy as jnp
from jax import lax
from jax.experimental import pallas as pl
from jax.experimental.pallas import tpu as pltpu
from jax.sharding import Mesh
from jax.sharding import PartitionSpec as P

CUTS = ("cuts_0", "cuts_1", "cuts_2")
ALL = (*CUTS, "site")
LANES = 128
COLUMNS = 256

coupling = 0.5
stepsize = 0.2


def stepped(field, momenta, start_force):
    half = momenta - 0.5 * stepsize * start_force
    return field + stepsize * half, half


def moved_by(trial, half, diagonal):
    force = trial - 2.0 * coupling * (1.0 - 2.0 * diagonal)
    return force, half - 0.5 * stepsize * force


def opening_kernel(field_ref, momenta_ref, start_ref, sent_ref, own_ref, held, sems):
    copies = [
        pltpu.make_async_copy(ref, held.at[k], sems.at[k])
        for k, ref in enumerate((field_ref, momenta_ref, start_ref))
    ]
    for copy in copies:
        copy.start()
    for copy in copies:
        copy.wait()
    field, momenta = held[0], held[1]
    trial, half = stepped(field, momenta, held[2])
    sent_ref[0:1, :] = trial
    sent_ref[1:2, :] = half
    own_ref[...] = trial * trial - momenta * momenta - field * field


def diagonal_kernel(nxt_ref, own_ref, near_ref, far_ref, forward_ref, back_ref,
                    diag_ref, part_ref, scaled, acc):
    rows, sites = forward_ref.shape
    blocks = rows // LANES
    site = lax.axis_index("site")
    first = site == 0

    def by_rows(row):
        whole = jnp.reshape(row, (2 * blocks, LANES))
        own = jnp.where(first, whole[:blocks], whole[blocks:])
        return own, jnp.where(first, whole[blocks:], whole[:blocks])

    growth = jnp.exp(coupling * nxt_ref[0:1, :])
    factors = jnp.transpose(jnp.concatenate(by_rows(growth), axis=0))
    near_at = pl.multiple_of(site * rows, LANES)
    far_at = pl.multiple_of((1 - site) * rows, LANES)

    def scale(j):
        span = pl.ds(j * COLUMNS, COLUMNS)
        for b in range(2 * blocks):
            source = near_ref if b < blocks else far_ref
            block = source[pl.ds(b % blocks * LANES, LANES), span].astype(jnp.float32)
            scaled[j % 2, pl.ds(b * LANES, LANES), :] = (factors[:, b : b + 1] * block).astype(jnp.bfloat16)

    steps = sites // COLUMNS
    scale(0)
    for j in range(steps):
        span = pl.ds(j * COLUMNS, COLUMNS)
        if j + 1 < steps:
            scale(j + 1)
        shrink = jnp.exp(-coupling * nxt_ref[0:1, span])
        wrapped = jnp.dot(
            forward_ref[:, pl.ds(near_at, rows)], scaled[j % 2, :rows, :], preferred_element_type=jnp.float32
        ) + jnp.dot(
            forward_ref[:, pl.ds(far_at, rows)], scaled[j % 2, rows:, :], preferred_element_type=jnp.float32
        )
        product = wrapped * (shrink * back_ref[:, span].astype(jnp.float32))
        part = product[:, :LANES] + product[:, LANES:]
        if j == 0:
            acc[...] = part
        else:
            acc[...] += part
    diag = jnp.concatenate(
        [
            jnp.sum(jnp.transpose(acc[pl.ds(b * LANES, LANES), :]), axis=0, keepdims=True)
            for b in range(blocks)
        ],
        axis=0,
    )
    diag_ref[...] = diag
    moved = moved_by(by_rows(nxt_ref[0:1, :])[0], by_rows(nxt_ref[1:2, :])[0], diag)[1]
    total = jnp.sum(moved * moved) + 0.5 * jnp.sum(own_ref[...])
    part_ref[...] = jnp.full(part_ref.shape, total, jnp.float32)


def closing_kernel(scale, accept_ref, field_ref, momenta_ref, start_ref, straight_ref, crossed_ref, parts_ref,
                   new_field_ref, new_momenta_ref, new_force_ref, change_ref):
    first = lax.axis_index("site") == 0
    straight, crossed = straight_ref[...], crossed_ref[...]
    diagonal = jnp.concatenate(
        [jnp.where(first, straight, crossed), jnp.where(first, crossed, straight)], axis=0
    )
    field = field_ref[...]
    trial, half = stepped(field, momenta_ref[...], start_ref[...])
    force, moved = moved_by(trial, half, jnp.reshape(diagonal, field.shape))
    new_force_ref[...] = force
    new_momenta_ref[...] = moved
    new_field_ref[...] = jnp.where(accept_ref[0] == 1, trial, field)
    change_ref[0] = scale * jnp.sum(parts_ref[...])


def on_device(field, momenta, start_force, green, forward_prop, back_prop, accept):
    near = green[0]
    rows, sites = near.shape
    devices = lax.axis_size(ALL)
    cuts = lax.axis_size(CUTS)
    row = jax.ShapeDtypeStruct((1, sites), jnp.float32)
    vmem = pl.BlockSpec(memory_space=pltpu.VMEM)
    smem = pl.BlockSpec(memory_space=pltpu.SMEM)

    def held(x):
        return pltpu.with_memory_space_constraint(x, pltpu.VMEM)

    far = lax.ppermute(near, "site", [(0, 1), (1, 0)])
    sent, own = pl.pallas_call(
        opening_kernel,
        out_shape=(pltpu.VMEM((2, sites), jnp.float32), pltpu.VMEM((1, sites), jnp.float32)),
        in_specs=[pl.BlockSpec(memory_space=pl.ANY)] * 3,
        out_specs=(vmem, vmem),
        scratch_shapes=[pltpu.VMEM((3, 1, sites), jnp.float32), pltpu.SemaphoreType.DMA((3,))],
        compiler_params=pltpu.CompilerParams(vmem_limit_bytes=1024 * 1024),
        cost_estimate=pl.CostEstimate(flops=8 * rows * sites * sites, bytes_accessed=8 * rows * sites, transcendentals=0),
        name="opening",
    )(*(pltpu.with_memory_space_constraint(x, pltpu.HBM) for x in (field, momenta, start_force)))
    nxt = lax.ppermute(sent, CUTS, [(i, (i - 1) % cuts) for i in range(cuts)])
    diag, part = pl.pallas_call(
        diagonal_kernel,
        out_shape=(
            jax.ShapeDtypeStruct((rows // LANES, LANES), jnp.float32),
            pltpu.VMEM((devices, LANES), jnp.float32),
        ),
        in_specs=[vmem] * 6,
        out_specs=(vmem, vmem),
        scratch_shapes=[
            pltpu.VMEM((2, sites, COLUMNS), jnp.bfloat16),
            pltpu.VMEM((rows, LANES), jnp.float32),
        ],
        compiler_params=pltpu.CompilerParams(vmem_limit_bytes=32 * 1024 * 1024),
        cost_estimate=pl.CostEstimate(
            flops=2 * rows * sites * sites, bytes_accessed=8 * rows * sites, transcendentals=2 * sites
        ),
        name="diagonal",
    )(*map(held, (nxt, own, near, far, forward_prop, back_prop)))
    straight = lax.ppermute(diag, ALL, [(i, (i + 2) % devices) for i in range(devices)])
    crossed = lax.ppermute(diag, ALL, [(i, ((i + 2) % devices) ^ 1) for i in range(devices)])
    parts = lax.all_to_all(part, ALL, split_axis=0, concat_axis=0, tiled=True)
    scale = 1.0 / (2.0 * (cuts * sites) ** 0.5) / LANES
    new_field, new_momenta, new_force, change = pl.pallas_call(
        lambda *refs: closing_kernel(scale, *refs),
        out_shape=(row, row, row, jax.ShapeDtypeStruct((1,), jnp.float32)),
        in_specs=[smem] + [vmem] * 6,
        out_specs=(vmem, vmem, vmem, smem),
        compiler_params=pltpu.CompilerParams(vmem_limit_bytes=4 * 1024 * 1024),
        name="closing",
    )(accept, *map(held, (field, momenta, start_force, straight, crossed, parts)))
    return new_field, new_momenta, new_force, change


def solution(mesh):
    finer = Mesh(
        mesh.devices.reshape(4, 8, 4, mesh.shape["site"]), ("cuts_0", "cuts_1", "cuts_2", "site")
    )
    in_specs = (
        P(CUTS, None),
        P(CUTS, None),
        P(CUTS, None),
        P(CUTS, "site", None),
        P("site", None),
        P("site", None),
        P(CUTS),
    )
    out_specs = (P(CUTS, None), P(CUTS, None), P(CUTS, None), P())
    return jax.shard_map(
        on_device, mesh=finer, in_specs=in_specs, out_specs=out_specs, check_vma=False
    )
```

```python
import jax
import jax.numpy as jnp
from jax import lax
from jax.experimental import pallas as pl
from jax.experimental.pallas import tpu as pltpu
from jax.sharding import Mesh
from jax.sharding import PartitionSpec as P

CUTS = ("cuts_0", "cuts_1", "cuts_2")
ALL = (*CUTS, "site")
LANES = 128
COLUMNS = 256

coupling = 0.5
stepsize = 0.2


def stepped(field, momenta, start_force):
    half = momenta - 0.5 * stepsize * start_force
    return field + stepsize * half, half


def moved_by(trial, half, diagonal):
    force = trial - 2.0 * coupling * (1.0 - 2.0 * diagonal)
    return force, half - 0.5 * stepsize * force


def opening_kernel(field_ref, momenta_ref, start_ref, own_ref, held, sems):
    copies = [
        pltpu.make_async_copy(ref, held.at[k], sems.at[k])
        for k, ref in enumerate((field_ref, momenta_ref, start_ref))
    ]
    for copy in copies:
        copy.start()
    for copy in copies:
        copy.wait()
    field, momenta = held[0], held[1]
    trial = stepped(field, momenta, held[2])[0]
    own_ref[...] = trial * trial - momenta * momenta - field * field


def diagonal_kernel(nxt_ref, own_ref, near_ref, far_ref, forward_ref, back_ref,
                    diag_ref, part_ref, scaled, acc):
    rows, sites = forward_ref.shape
    blocks = rows // LANES
    site = lax.axis_index("site")
    first = site == 0

    def by_rows(row):
        whole = jnp.reshape(row, (2 * blocks, LANES))
        own = jnp.where(first, whole[:blocks], whole[blocks:])
        return own, jnp.where(first, whole[blocks:], whole[:blocks])

    base = 0.5 * jnp.sum(own_ref[...])
    growth = jnp.exp(coupling * nxt_ref[0:1, :])
    factors = jnp.transpose(jnp.concatenate(by_rows(growth), axis=0))
    near_at = pl.multiple_of(site * rows, LANES)
    far_at = pl.multiple_of((1 - site) * rows, LANES)

    def scale(j):
        span = pl.ds(j * COLUMNS, COLUMNS)
        for b in range(2 * blocks):
            source = near_ref if b < blocks else far_ref
            block = source[pl.ds(b % blocks * LANES, LANES), span].astype(jnp.float32)
            scaled[j % 2, pl.ds(b * LANES, LANES), :] = (factors[:, b : b + 1] * block).astype(jnp.bfloat16)

    steps = sites // COLUMNS
    scale(0)
    for j in range(steps):
        span = pl.ds(j * COLUMNS, COLUMNS)
        if j + 1 < steps:
            scale(j + 1)
        shrink = jnp.exp(-coupling * nxt_ref[0:1, span])
        wrapped = jnp.dot(
            forward_ref[:, pl.ds(near_at, rows)], scaled[j % 2, :rows, :], preferred_element_type=jnp.float32
        ) + jnp.dot(
            forward_ref[:, pl.ds(far_at, rows)], scaled[j % 2, rows:, :], preferred_element_type=jnp.float32
        )
        product = wrapped * (shrink * back_ref[:, span].astype(jnp.float32))
        part = product[:, :LANES] + product[:, LANES:]
        if j == 0:
            acc[...] = part
        else:
            acc[...] += part
    diag = jnp.concatenate(
        [
            jnp.sum(jnp.transpose(acc[pl.ds(b * LANES, LANES), :]), axis=0, keepdims=True)
            for b in range(blocks)
        ],
        axis=0,
    )
    diag_ref[...] = diag
    moved = moved_by(by_rows(nxt_ref[0:1, :])[0], by_rows(nxt_ref[1:2, :])[0], diag)[1]
    total = jnp.sum(moved * moved) + base
    part_ref[...] = jnp.full(part_ref.shape, total, jnp.float32)


def closing_kernel(scale, accept_ref, field_ref, momenta_ref, start_ref, straight_ref, crossed_ref, parts_ref,
                   new_field_ref, new_momenta_ref, new_force_ref, change_ref):
    first = lax.axis_index("site") == 0
    straight, crossed = straight_ref[...], crossed_ref[...]
    diagonal = jnp.concatenate(
        [jnp.where(first, straight, crossed), jnp.where(first, crossed, straight)], axis=0
    )
    field = field_ref[...]
    trial, half = stepped(field, momenta_ref[...], start_ref[...])
    force, moved = moved_by(trial, half, jnp.reshape(diagonal, field.shape))
    new_force_ref[...] = force
    new_momenta_ref[...] = moved
    new_field_ref[...] = jnp.where(accept_ref[0] == 1, trial, field)
    change_ref[0] = scale * jnp.sum(parts_ref[...])


def on_device(field, momenta, start_force, green, forward_prop, back_prop, accept):
    near = green[0]
    rows, sites = near.shape
    devices = lax.axis_size(ALL)
    cuts = lax.axis_size(CUTS)
    row = jax.ShapeDtypeStruct((1, sites), jnp.float32)
    vmem = pl.BlockSpec(memory_space=pltpu.VMEM)
    smem = pl.BlockSpec(memory_space=pltpu.SMEM)

    def held(x):
        return pltpu.with_memory_space_constraint(x, pltpu.VMEM)

    sent = jnp.concatenate(stepped(field, momenta, start_force), axis=0)
    nxt = lax.ppermute(sent, ALL, [(i, ((i - 2) % devices) ^ 1) for i in range(devices)])
    far = lax.ppermute(near, "site", [(0, 1), (1, 0)])
    own = pl.pallas_call(
        opening_kernel,
        out_shape=pltpu.VMEM((1, sites), jnp.float32),
        in_specs=[pl.BlockSpec(memory_space=pl.ANY)] * 3,
        out_specs=vmem,
        scratch_shapes=[pltpu.VMEM((3, 1, sites), jnp.float32), pltpu.SemaphoreType.DMA((3,))],
        compiler_params=pltpu.CompilerParams(vmem_limit_bytes=1024 * 1024),
        cost_estimate=pl.CostEstimate(flops=8 * rows * sites * sites, bytes_accessed=8 * rows * sites, transcendentals=0),
        name="opening",
    )(*(pltpu.with_memory_space_constraint(x, pltpu.HBM) for x in (field, momenta, start_force)))
    diag, part = pl.pallas_call(
        diagonal_kernel,
        out_shape=(
            jax.ShapeDtypeStruct((rows // LANES, LANES), jnp.float32),
            pltpu.VMEM((devices, LANES), jnp.float32),
        ),
        in_specs=[vmem] * 6,
        out_specs=(vmem, vmem),
        scratch_shapes=[
            pltpu.VMEM((2, sites, COLUMNS), jnp.bfloat16),
            pltpu.VMEM((rows, LANES), jnp.float32),
        ],
        compiler_params=pltpu.CompilerParams(vmem_limit_bytes=32 * 1024 * 1024),
        cost_estimate=pl.CostEstimate(
            flops=2 * rows * sites * sites, bytes_accessed=8 * rows * sites, transcendentals=2 * sites
        ),
        name="diagonal",
    )(*map(held, (nxt, own, near, far, forward_prop, back_prop)))
    straight = lax.ppermute(diag, ALL, [(i, (i + 2) % devices) for i in range(devices)])
    crossed = lax.ppermute(diag, ALL, [(i, ((i + 2) % devices) ^ 1) for i in range(devices)])
    parts = lax.all_to_all(part, ALL, split_axis=0, concat_axis=0, tiled=True)
    scale = 1.0 / (2.0 * (cuts * sites) ** 0.5) / LANES
    new_field, new_momenta, new_force, change = pl.pallas_call(
        lambda *refs: closing_kernel(scale, *refs),
        out_shape=(row, row, row, jax.ShapeDtypeStruct((1,), jnp.float32)),
        in_specs=[smem] + [vmem] * 6,
        out_specs=(vmem, vmem, vmem, smem),
        compiler_params=pltpu.CompilerParams(vmem_limit_bytes=4 * 1024 * 1024),
        name="closing",
    )(accept, *map(held, (field, momenta, start_force, straight, crossed, parts)))
    return new_field, new_momenta, new_force, change


def solution(mesh):
    finer = Mesh(
        mesh.devices.reshape(4, 8, 4, mesh.shape["site"]), ("cuts_0", "cuts_1", "cuts_2", "site")
    )
    in_specs = (
        P(CUTS, None),
        P(CUTS, None),
        P(CUTS, None),
        P(CUTS, "site", None),
        P("site", None),
        P("site", None),
        P(CUTS),
    )
    out_specs = (P(CUTS, None), P(CUTS, None), P(CUTS, None), P())
    return jax.shard_map(
        on_device, mesh=finer, in_specs=in_specs, out_specs=out_specs, check_vma=False
    )
```
